512 devices in a mesh: fsdp: 128 (over y, z_lo, x), dp: 4 (over z_hi, core).
Axes of the slice: x: 4, y: 4, z: 16 (z_hi: 2, z_lo: 8; z = z_hi * 8 + z_lo), core: 2. Of those that a mesh axis runs over, the one named last changes fastest.
Arguments:
- tokens: bfloat16 [65536, 4096], P(('fsdp', 'dp')), may hold values from -6 to 6
- norm_gain: float32 [4096], replicated, may hold values from 0.25 to 1.75
- penalty: float32 [14336], P('dp'), may hold values from 0.25 to 4
- weight_tiles: bfloat16 [4, 384, 4096], P(None, 'fsdp'), may hold values from -0.375 to 0.375
- block_rows: int32 [224, 4], replicated, may hold values from 0 to 63, as said below
- block_slot: int32 [224, 4], replicated, may hold values from 0 to 383, as said below
Outputs:
- grad_tokens: bfloat16 [65536, 4096], P(('fsdp', 'dp'))
The draws below stay inside these ranges and needn't reach their ends.
Inputs may be any that keep to these rules, and one draw needn't show every extreme that they name: `block_rows`: each block column names 4 distinct block rows. Within each run of 56 block columns (columns q * 56 to (q + 1) * 56 - 1), a block row is named at most 4 times, and some block row exactly 4 times. `block_slot`: within each run of 56 block columns, no slot is named twice. Slot s is stored by fsdp index s // 3; in each run some fsdp index has all 3 of its slots named.
All inputs are finite; a program needn't handle non-finite values.
Results may differ from the reference program's by a relative error of at most 0.014.
Values may be sent and summed in bfloat16 or wider, within the bound.
No kernel may reach another device: no remote copies, remote signals or barrier semaphores. Data moves between devices by JAX's collectives and lax.ppermute only.
A program may use at most 128 MiB of HBM per device.

```python
import math
import jax
import jax.numpy as jnp
from jax import lax

D = 4096
FF = 14336
BLOCK = 64
KB = 4
NRB = 64
FFB = 224
QUARTERS = 4
FQB = 56
SLOTS = 3
SLOTS_ALL = 384
ROWS = 512
TOKENS = 65536
N_FSDP = 128


def draw_block_rows(key, part):
    pieces = []
    for quarter in range(QUARTERS):
        sub_key = jax.random.fold_in(key, 101 + quarter)
        first_key, second_key = jax.random.split(sub_key)
        row_order = jax.random.permutation(first_key, NRB).astype(jnp.int32)
        column_order = jax.random.permutation(second_key, FQB).astype(jnp.int32)
        position = (column_order[:, None] * KB + jnp.arange(KB, dtype=jnp.int32)[None, :]) % NRB
        pieces.append(row_order[position])
    return jnp.concatenate(pieces, 0).astype(jnp.int32)


def draw_block_slot(key, part):
    owners = SLOTS_ALL // SLOTS
    pieces = []
    for quarter in range(QUARTERS):
        sub_key = jax.random.fold_in(key, 211 + quarter)
        heat_key, hot_key, order_key, shuffle_key = jax.random.split(sub_key, 4)
        heat_level = jax.random.randint(heat_key, (owners,), 1, 5).astype(jnp.int32)
        hottest = jax.random.randint(hot_key, (), 0, owners).astype(jnp.int32)
        slot_level = jnp.arange(SLOTS, dtype=jnp.int32)[None, :] * 16 // heat_level[:, None] + 1
        slot_level = jnp.where(jnp.arange(owners, dtype=jnp.int32)[:, None] == hottest, 0, slot_level)
        tie_order = jax.random.permutation(order_key, SLOTS_ALL).astype(jnp.int32).reshape(owners, SLOTS)
        sort_keys = (slot_level * SLOTS_ALL + tie_order).reshape(-1)
        unused_values, chosen = lax.top_k(-sort_keys, FQB * KB)
        shuffled = jax.random.permutation(shuffle_key, chosen.astype(jnp.int32))
        pieces.append(shuffled.reshape(FQB, KB))
    return jnp.concatenate(pieces, 0).astype(jnp.int32)


def level_of(key, shape, cuts, least, top_value):
    factor_of, own = 1.0, jax.random.fold_in(key, 6)
    for dim, parts in cuts:
        draws = jnp.exp(jax.random.uniform(jax.random.fold_in(own, dim), (parts,), jnp.float32, least / len(cuts), top_value / len(cuts)))
        factor_of = factor_of * jnp.repeat(draws, shape[dim] // parts).reshape([-1 if axis == dim else 1 for axis in range(len(shape))])
    return factor_of


def noise(key, shape, scale, bound, cuts=(), kind=jnp.bfloat16):
    gain = level_of(key, shape, cuts, -0.22, 0.18) if cuts else 1.0
    array = jax.random.normal(key, shape, jnp.float32) * scale * gain
    return jnp.minimum(jnp.maximum(array, -bound), bound).astype(kind)


def setup_inputs(seed: int = 0) -> dict:
    key_list = jax.random.split(jax.random.key(seed), 7)
    return {
        "tokens": noise(key_list[0], (TOKENS, D), 1.0, 6.0, ((0, 512),)),
        "norm_gain": jnp.clip(1.0 + 0.15 * jax.random.normal(key_list[1], (D,), jnp.float32), 0.25, 1.75),
        "penalty": jnp.clip(jnp.exp(math.log(4.0) - 2.7725887 * jax.random.uniform(key_list[2], (FF,), jnp.float32) ** level_of(key_list[2], (FF,), ((0, 4),), -0.2, 0.2)), 0.25, 4.0),
        "weight_tiles": noise(key_list[3], (QUARTERS, SLOTS_ALL, BLOCK * BLOCK), (KB * BLOCK) ** -0.5, 0.375, ((1, 128),)),
        "block_rows": draw_block_rows(jax.random.fold_in(key_list[6], 71), 0),
        "block_slot": draw_block_slot(jax.random.fold_in(key_list[6], 71), 0),
    }


def reference(tokens, norm_gain, penalty, weight_tiles, block_rows, block_slot):
    quarter_of = (jnp.arange(FFB, dtype=jnp.int32) // FQB).astype(jnp.int32)
    picked = weight_tiles[quarter_of[:, None], block_slot]
    all_weights = picked.astype(jnp.float32).reshape(FFB, KB, BLOCK, BLOCK)

    def one_group(group_index):
        row_start = (group_index * ROWS).astype(jnp.int32)
        group_tokens = lax.dynamic_slice_in_dim(tokens, row_start, ROWS, 0).astype(jnp.float32)
        rms_scale = jnp.sqrt(lax.optimization_barrier(jnp.mean(group_tokens * group_tokens, axis=1, keepdims=True)) + 1e-05)
        normed = group_tokens / rms_scale
        scaled = (normed * norm_gain).astype(jnp.bfloat16)
        feat_blocks = scaled.astype(jnp.float32).T.reshape(NRB, BLOCK, ROWS)
        grad_total = jnp.zeros((NRB, BLOCK, ROWS), jnp.float32)
        for quarter in range(QUARTERS):
            weights_here = all_weights[quarter * FQB:(quarter + 1) * FQB]
            rows_here = block_rows[quarter * FQB:(quarter + 1) * FQB]
            unit_scale = penalty[quarter * FQB * BLOCK:(quarter + 1) * FQB * BLOCK].reshape(FQB, BLOCK, 1)
            selected = feat_blocks[rows_here]
            preact = jnp.einsum('ckio,ckin->con', weights_here, selected)
            gating = jax.nn.sigmoid(preact)
            grad_act = unit_scale * (preact * gating)
            grad_pre = (grad_act * (gating * (1.0 + preact * (1.0 - gating)))).astype(jnp.bfloat16)
            block_terms = jnp.einsum('ckio,con->ckin', weights_here, grad_pre.astype(jnp.float32))
            summed = jax.ops.segment_sum(block_terms.reshape(FQB * KB, BLOCK, ROWS), rows_here.reshape(-1), num_segments=NRB)
            grad_total = grad_total + summed.astype(jnp.bfloat16).astype(jnp.float32)
        grad_scaled = grad_total.reshape(D, ROWS).T
        grad_norm = grad_scaled * norm_gain
        mixing = lax.optimization_barrier(jnp.mean(grad_norm * normed, axis=1, keepdims=True))
        return ((grad_norm - normed * mixing) / rms_scale).astype(jnp.bfloat16)
    result = lax.map(one_group, jnp.arange(N_FSDP, dtype=jnp.int32))
    return result.reshape(TOKENS, D)
```

```python
import jax
import jax.numpy as jnp
from jax import lax
from jax.experimental import pallas as pl
from jax.experimental.pallas import tpu as pltpu
from jax.sharding import Mesh
from jax.sharding import PartitionSpec as P

BLOCK = 64
HALF = BLOCK // 2
EPS = 1e-05
LANES = 128
GROUP = 8
NX, NY, NZ = 4, 4, 8
SIDE = 4
AXES = ("y", "zl", "x", "zh", "core")


def norm_kernel(tokens_ref, gain_ref, feat_ref, inverse_ref):
    x = tokens_ref[...].astype(jnp.float32)
    inverse = 1.0 / jnp.sqrt(jnp.mean(x * x, axis=1, keepdims=True) + EPS)
    inverse_ref[...] = inverse
    scaled = ((x * inverse) * gain_ref[...]).astype(jnp.bfloat16)
    for at in range(0, x.shape[1], LANES):
        feat_ref[at : at + LANES, :] = scaled[:, at : at + LANES].T


def sparse_kernel(columns, per_column, pieces, refs):
    tile_ref, row_ref, unit_ref, mine_ref, other_ref = refs[:5]
    parts = refs[5 : 5 + len(pieces)]
    keep_ref, send_ref, away_ref, w_ref, sems = refs[5 + len(pieces) :]
    count = mine_ref.shape[2]

    copies = []
    for i, (run, start, size) in enumerate(pieces):
        copies.append(
            pltpu.make_async_copy(parts[i], w_ref.at[run, pl.ds(start, size)], sems.at[i])
        )
    for copy in copies:
        copy.start()
    keep_ref[...] = jnp.zeros_like(keep_ref)
    away_ref[...] = jnp.zeros_like(away_ref)
    blank = jnp.zeros((BLOCK, 2 * count), jnp.bfloat16)

    def work(run):
        def group(g, carry):
            first = (run * columns + g * GROUP) * per_column
            units = unit_ref[run, g]

            def forward(j):
                at = first + j * per_column
                rows = [row_ref[at + k] for k in range(per_column)]
                stack = jnp.concatenate(
                    [w_ref[run, tile_ref[at + k]] for k in range(per_column)], axis=0
                )
                turned = stack.T
                lhs = jnp.concatenate([turned[:BLOCK], turned[BLOCK:]], axis=1)
                mine = [mine_ref[r] for r in rows]
                other = [other_ref[r] for r in rows]
                rhs = jnp.concatenate(
                    [
                        jnp.concatenate([p[:HALF] for p in side] + [p[HALF:] for p in side], axis=0)
                        for side in (mine, other)
                    ],
                    axis=1,
                )
                preact = jnp.dot(lhs, rhs, preferred_element_type=jnp.float32)
                gating = jax.nn.sigmoid(preact)
                grad_act = units[:, j : j + 1] * (preact * gating)
                grad_pre = grad_act * (gating * (1.0 + preact * (1.0 - gating)))
                return rows, stack, grad_pre.astype(jnp.bfloat16)

            def backward(rows, stack, grad_pre):
                upper = jnp.dot(
                    stack,
                    jnp.concatenate([grad_pre, blank], axis=0),
                    preferred_element_type=jnp.float32,
                )
                lower = jnp.dot(
                    stack,
                    jnp.concatenate([blank, grad_pre], axis=0),
                    preferred_element_type=jnp.float32,
                )
                for ref, lanes in ((keep_ref, slice(0, count)), (away_ref, slice(count, None))):
                    sums = []
                    for k in range(per_column):
                        span = slice(k * HALF, (k + 1) * HALF)
                        term = jnp.concatenate([upper[span, lanes], lower[span, lanes]], axis=0)
                        sums.append(ref[rows[k]] + term)
                    for k in range(per_column):
                        ref[rows[k]] = sums[k]

            held = [forward(j) for j in range(GROUP)]
            for piece in held:
                backward(*piece)
            return carry

        lax.fori_loop(0, columns // GROUP, group, 0)

    for run in range(2):
        for copy, piece in zip(copies, pieces):
            if piece[0] == run:
                copy.wait()
        work(run)
    send_ref[...] = away_ref[...].astype(jnp.bfloat16)


def close_kernel(keep_ref, came_ref, tokens_ref, gain_ref, inverse_ref, out_ref, grad_ref):
    inverse = inverse_ref[...]
    width = tokens_ref.shape[1]
    total = jnp.zeros((tokens_ref.shape[0], LANES), jnp.float32)
    for at in range(0, width, LANES):
        span = slice(at, at + LANES)
        grad = (keep_ref[span, :] + came_ref[span, :].astype(jnp.float32)).T
        grad = grad * gain_ref[:, span]
        grad_ref[:, span] = grad
        total += grad * (tokens_ref[:, span].astype(jnp.float32) * inverse)
    mixing = jnp.sum(total, axis=1, keepdims=True) * (1.0 / width)
    for at in range(0, width, LANES):
        span = slice(at, at + LANES)
        normed = tokens_ref[:, span].astype(jnp.float32) * inverse
        out_ref[:, span] = ((grad_ref[:, span] - normed * mixing) * inverse).astype(jnp.bfloat16)


def along_z(v, step):
    size = 2 * NZ
    at = lambda z: (z % NZ) * 2 + z // NZ
    return lax.ppermute(v, ("zl", "zh"), [(at(z), at((z + step) % size)) for z in range(size)])


def along_side(v, step, leg):
    pairs = []
    for y in range(NY):
        for x in range(NX):
            for core in range(2):
                to_y, to_x = (y, (x + step) % NX) if core == leg else ((y + step) % NY, x)
                pairs.append(((y * NX + x) * 2 + core, (to_y * NX + to_x) * 2 + core))
    return lax.ppermute(v, ("y", "x", "core"), pairs)


def swap_cores(v):
    return lax.ppermute(v, "core", [(0, 1), (1, 0)])


def gather_tiles(own):
    slots = own.shape[1]
    own = own[:, None]
    below, above = along_z(own, 1), along_z(own, -1)
    near = jnp.concatenate([below, own, above], axis=1)
    far_below = along_z(near, 3)
    far_above = along_z(near[:, :2], -3)
    line = jnp.concatenate([own, above, far_above, far_below, below], axis=1)
    line = line.reshape(2, NZ * slots, HALF, 2 * BLOCK)
    back, ahead = along_side(line, 1, 0), along_side(line, -1, 0)
    across = (along_side(back[0], 1, 0), along_side(ahead[1], -1, 0))
    found = []
    for run in range(2):
        plane = jnp.concatenate([line[run], ahead[run], across[run], back[run]], axis=0)
        found.append((plane, along_side(plane, 1, 1), along_side(plane, -1, 1)))
    pieces, arrays = [], []
    for run, (plane, back, ahead) in enumerate(found):
        size = plane.shape[0]
        half = size // 2
        from_back = along_side(back[:half], 1, 1)
        from_ahead = along_side(ahead[half:], -1, 1)
        pieces += [
            (run, 0, size),
            (run, size, size),
            (run, 2 * size, half),
            (run, 2 * size + half, half),
            (run, 3 * size, size),
        ]
        arrays += [plane, ahead, from_back, from_ahead, back]
    return pieces, arrays


def tile_places(block_slot, slots, y, zl, x, core):
    owner, place = block_slot // slots, block_slot % slots
    step_x = (owner % NX - x) % NX
    step_z = ((owner // NX) % NZ - zl) % NZ
    step_y = (owner // (NX * NZ) - y) % NY
    first = jnp.where(core == 0, step_x, step_y)
    second = jnp.where(core == 0, step_y, step_x)
    return ((second * SIDE + first) * NZ + step_z) * slots + place


def sparse_call(places, rows, units, mine, other, pieces, arrays):
    row_blocks, _, count = mine.shape
    columns, per_column = rows.shape[1:]
    tiles = SIDE * SIDE * NZ * (arrays[0].shape[0] // (SIDE * NZ))

    def body(*refs):
        sparse_kernel(columns, per_column, pieces, refs)

    smem = pl.BlockSpec(memory_space=pltpu.SMEM)
    vmem = pl.BlockSpec(memory_space=pltpu.VMEM)
    anywhere = pl.BlockSpec(memory_space=pl.ANY)
    return pl.pallas_call(
        body,
        out_shape=(
            jax.ShapeDtypeStruct((row_blocks, BLOCK, count), jnp.float32),
            jax.ShapeDtypeStruct((row_blocks, BLOCK, count), jnp.bfloat16),
        ),
        in_specs=[smem, smem, vmem, vmem, vmem] + [anywhere] * len(arrays),
        out_specs=(vmem, vmem),
        scratch_shapes=[
            pltpu.VMEM((row_blocks, BLOCK, count), jnp.float32),
            pltpu.VMEM((2, tiles, HALF, 2 * BLOCK), jnp.bfloat16),
            pltpu.SemaphoreType.DMA((len(arrays),)),
        ],
    )(places.reshape(-1), rows.reshape(-1), units, mine, other, *arrays)


def norm_call(tokens, gain):
    count, width = tokens.shape
    return pl.pallas_call(
        norm_kernel,
        out_shape=(
            jax.ShapeDtypeStruct((width, count), jnp.bfloat16),
            jax.ShapeDtypeStruct((count, 1), jnp.float32),
        ),
    )(tokens, gain)


def close_call(keep, came, tokens, gain, inverse):
    count, width = tokens.shape
    return pl.pallas_call(
        close_kernel,
        out_shape=jax.ShapeDtypeStruct((count, width), jnp.bfloat16),
        scratch_shapes=[pltpu.VMEM((count, width), jnp.float32)],
    )(keep.reshape(width, count), came.reshape(width, count), tokens, gain, inverse)


def unit_table(penalty, columns):
    return penalty.reshape(-1, columns // GROUP, GROUP, BLOCK).transpose(0, 1, 3, 2)


def pack_tiles(tiles):
    lead = tiles.shape[:-1]
    split = tiles.reshape(*lead, 2, HALF, BLOCK)
    return jnp.moveaxis(split, -3, -2).reshape(*lead, HALF, 2 * BLOCK)


def on_device(tokens, norm_gain, penalty, weight_tiles, block_rows, block_slot):
    y, zl, x, zh, core = (lax.axis_index(name) for name in AXES)
    runs, slots, tile_size = weight_tiles.shape
    count, width = tokens.shape
    columns, per_column = block_rows.shape[0] // runs, block_rows.shape[1]

    def of_core(table):
        paired = table.reshape(2, 2, *table.shape[1:])
        return lax.dynamic_index_in_dim(paired, core, 1, keepdims=False)

    own = pack_tiles(of_core(weight_tiles))
    pieces, arrays = gather_tiles(own)
    far_penalty = lax.ppermute(penalty, "zh", [(0, 1), (1, 0)])
    both = jnp.stack(
        [jnp.where(zh == 0, penalty, far_penalty), jnp.where(zh == 0, far_penalty, penalty)]
    )
    rows = of_core(block_rows.reshape(runs, columns, per_column))
    places = of_core(
        tile_places(block_slot, slots, y, zl, x, core).reshape(runs, columns, per_column)
    )
    gain = norm_gain.reshape(1, width)
    features, inverse = norm_call(tokens, gain)
    other = swap_cores(features)
    blocks = (width // BLOCK, BLOCK, count)
    keep, send = sparse_call(
        places, rows, unit_table(both, columns), features.reshape(blocks), other.reshape(blocks),
        pieces, arrays,
    )
    came = swap_cores(send)
    return close_call(keep, came, tokens, gain, inverse)


def solution(mesh):
    fine = Mesh(mesh.devices.reshape(NY, NZ, NX, 2, 2), AXES)
    placed = (P(AXES, None), P(), P(("zh", "core")), P(None, ("y", "zl", "x"), None), P(), P())
    return jax.shard_map(
        on_device, mesh=fine, in_specs=placed, out_specs=P(AXES, None), check_vma=False
    )
```

```python
import jax
import jax.numpy as jnp
from jax import lax
from jax.experimental import pallas as pl
from jax.experimental.pallas import tpu as pltpu
from jax.sharding import Mesh
from jax.sharding import PartitionSpec as P

BLOCK = 64
HALF = BLOCK // 2
EPS = 1e-05
LANES = 128
GROUP = 8
NX, NY, NZ = 4, 4, 8
SIDE = 4
AXES = ("y", "zl", "x", "zh", "core")
SMEM = pl.BlockSpec(memory_space=pltpu.SMEM)
VMEM = pl.BlockSpec(memory_space=pltpu.VMEM)


def on_chip(x):
    return pltpu.with_memory_space_constraint(x, pltpu.VMEM)


def norm_kernel(tokens_ref, gain_ref, feat_ref, inverse_ref):
    x = tokens_ref[...].astype(jnp.float32)
    inverse = 1.0 / jnp.sqrt(jnp.mean(x * x, axis=1, keepdims=True) + EPS)
    inverse_ref[...] = inverse
    scaled = ((x * inverse) * gain_ref[...]).astype(jnp.bfloat16)
    for at in range(0, x.shape[1], LANES):
        feat_ref[at : at + LANES, :] = scaled[:, at : at + LANES].T


def sparse_kernel(columns, per_column, tile_ref, row_ref, unit_ref, mine_ref, other_ref, *refs):
    parts, (keep_ref, send_ref, away_ref, w_ref, sems) = refs[:8], refs[8:]
    count = mine_ref.shape[2]
    size = parts[0].shape[0]
    copies = []
    for i, source in enumerate(parts):
        run, at = i // SIDE, i % SIDE
        target = w_ref.at[run, pl.ds(at * size, size)]
        copies.append(pltpu.make_async_copy(source, target, sems.at[run, at]))
    for copy in copies:
        copy.start()
    keep_ref[...] = jnp.zeros_like(keep_ref)
    away_ref[...] = jnp.zeros_like(away_ref)
    blank = jnp.zeros((BLOCK, 2 * count), jnp.bfloat16)

    def work(run):
        def group(g, carry):
            first = (run * columns + g * GROUP) * per_column
            units = unit_ref[run, g]

            def forward(j):
                at = first + j * per_column
                rows = [row_ref[at + k] for k in range(per_column)]
                stack = jnp.concatenate(
                    [w_ref[run, tile_ref[at + k]] for k in range(per_column)], axis=0
                )
                turned = stack.T
                lhs = jnp.concatenate([turned[:BLOCK], turned[BLOCK:]], axis=1)
                mine = [mine_ref[r] for r in rows]
                other = [other_ref[r] for r in rows]
                rhs = jnp.concatenate(
                    [
                        jnp.concatenate([p[:HALF] for p in side] + [p[HALF:] for p in side], axis=0)
                        for side in (mine, other)
                    ],
                    axis=1,
                )
                preact = jnp.dot(lhs, rhs, preferred_element_type=jnp.float32)
                gating = jax.nn.sigmoid(preact)
                grad_act = units[:, j : j + 1] * (preact * gating)
                grad_pre = grad_act * (gating * (1.0 + preact * (1.0 - gating)))
                return rows, stack, grad_pre.astype(jnp.bfloat16)

            def backward(rows, stack, grad_pre):
                upper = jnp.dot(
                    stack,
                    jnp.concatenate([grad_pre, blank], axis=0),
                    preferred_element_type=jnp.float32,
                )
                lower = jnp.dot(
                    stack,
                    jnp.concatenate([blank, grad_pre], axis=0),
                    preferred_element_type=jnp.float32,
                )
                for ref, lanes in ((keep_ref, slice(0, count)), (away_ref, slice(count, None))):
                    sums = []
                    for k in range(per_column):
                        span = slice(k * HALF, (k + 1) * HALF)
                        term = jnp.concatenate([upper[span, lanes], lower[span, lanes]], axis=0)
                        sums.append(ref[rows[k]] + term)
                    for k in range(per_column):
                        ref[rows[k]] = sums[k]

            held = [forward(j) for j in range(GROUP)]
            for piece in held:
                backward(*piece)
            return carry

        lax.fori_loop(0, columns // GROUP, group, 0)

    for run in range(2):
        for copy in copies[4 * run : 4 * run + 4]:
            copy.wait()
        work(run)
    send_ref[...] = away_ref[...].astype(jnp.bfloat16)


def close_kernel(keep_ref, came_ref, tokens_ref, gain_ref, inverse_ref, out_ref, grad_ref):
    inverse = inverse_ref[...]
    width = tokens_ref.shape[1]
    total = jnp.zeros((tokens_ref.shape[0], LANES), jnp.float32)
    for at in range(0, width, LANES):
        span = slice(at, at + LANES)
        grad = (keep_ref[span, :] + came_ref[span, :].astype(jnp.float32)).T
        grad = grad * gain_ref[:, span]
        grad_ref[:, span] = grad
        total += grad * (tokens_ref[:, span].astype(jnp.float32) * inverse)
    mixing = jnp.sum(total, axis=1, keepdims=True) * (1.0 / width)
    for at in range(0, width, LANES):
        span = slice(at, at + LANES)
        normed = tokens_ref[:, span].astype(jnp.float32) * inverse
        out_ref[:, span] = ((grad_ref[:, span] - normed * mixing) * inverse).astype(jnp.bfloat16)


def along_z(v, step):
    size = 2 * NZ
    pairs = []
    for z in range(size):
        for core in range(2):
            to = (z + (step if core == 0 else -step)) % size
            pairs.append([((at % NZ) * 2 + at // NZ) * 2 + core for at in (z, to)])
    return lax.ppermute(v, ("zl", "zh", "core"), pairs)


def along_side(v, step, leg):
    pairs = []
    for y in range(NY):
        for x in range(NX):
            for core in range(2):
                to_y, to_x = (y, (x + step) % NX) if core == leg else ((y + step) % NY, x)
                pairs.append(((y * NX + x) * 2 + core, (to_y * NX + to_x) * 2 + core))
    return lax.ppermute(v, ("y", "x", "core"), pairs)


def swap_cores(v):
    return lax.ppermute(v, "core", [(0, 1), (1, 0)])


def join_kernel(line_ref, ahead_ref, across_ref, back_ref, *plane_refs):
    size = line_ref.shape[1]
    for run, plane_ref in enumerate(plane_refs):
        for i, ref in enumerate((line_ref, ahead_ref, across_ref, back_ref)):
            plane_ref[i * size : (i + 1) * size] = ref[run]


def join(*parts):
    runs, size, *tile = parts[0].shape
    return pl.pallas_call(
        join_kernel,
        out_shape=[pltpu.VMEM((SIDE * size, *tile), parts[0].dtype)] * runs,
        in_specs=[VMEM] * len(parts),
        out_specs=[VMEM] * runs,
        compiler_params=pltpu.CompilerParams(vmem_limit_bytes=1 << 20),
    )(*map(on_chip, parts))


def of_core(table, core):
    paired = table.reshape(*table.shape[:-4], 2, 2, *table.shape[-3:])
    return lax.dynamic_index_in_dim(paired, core, paired.ndim - 4, keepdims=False)


def gather_tiles(own, core, early):
    _, slots = own.shape[:2]
    mine = of_core(own, core)
    far = along_z(own, 3)
    opposite = along_z(mine, 4)
    middle = along_z(own, 2)
    near = along_z(own, 1)
    near, middle, far, early = lax.optimization_barrier((near, middle, far, early))
    side = jnp.stack([near, middle, far])
    theirs = swap_cores(of_core(side, 1 - core))
    line = jnp.concatenate([mine[None], of_core(side, core), opposite[None], theirs], axis=0)
    line = line.transpose(1, 0, 2, 3, 4).reshape(2, NZ * slots, HALF, 2 * BLOCK)
    across, back, ahead = along_side(line, 2, 0), along_side(line, 1, 0), along_side(line, -1, 0)
    planes = join(line, ahead, across, back)
    back_0, ahead_1 = along_side(planes[0], 1, 1), along_side(planes[1], -1, 1)
    back_1, ahead_0 = along_side(planes[1], 1, 1), along_side(planes[0], -1, 1)
    across_0, across_1 = along_side(back_0, 1, 1), along_side(ahead_1, -1, 1)
    pieces = [planes[0], ahead_0, across_0, back_0, planes[1], ahead_1, across_1, back_1]
    return pieces, early


def tile_places(block_slot, slots, y, zl, x, core):
    owner, place = block_slot // slots, block_slot % slots
    step_x = (owner % NX - x) % NX
    step_z = ((owner // NX) % NZ - zl) * (2 * core - 1) % NZ
    step_z = jnp.where(step_z > NZ // 2, 3 * NZ // 2 - step_z, step_z)
    step_y = (owner // (NX * NZ) - y) % NY
    first = jnp.where(core == 0, step_x, step_y)
    second = jnp.where(core == 0, step_y, step_x)
    return ((second * SIDE + first) * NZ + step_z) * slots + place


def sparse_call(columns, per_column, places, rows, units, mine, other, tiles):
    row_blocks, _, count = mine.shape

    def body(*refs):
        sparse_kernel(columns, per_column, *refs)

    return pl.pallas_call(
        body,
        out_shape=(
            pltpu.VMEM((row_blocks, BLOCK, count), jnp.float32),
            pltpu.VMEM((row_blocks, BLOCK, count), jnp.bfloat16),
        ),
        in_specs=[SMEM, SMEM] + [VMEM] * 11,
        out_specs=(VMEM, VMEM),
        scratch_shapes=[
            pltpu.VMEM((row_blocks, BLOCK, count), jnp.float32),
            pltpu.VMEM((2, SIDE * tiles[0].shape[0], HALF, 2 * BLOCK), jnp.bfloat16),
            pltpu.SemaphoreType.DMA((2, 4)),
        ],
        compiler_params=pltpu.CompilerParams(vmem_limit_bytes=14 << 20),
    )(
        places, rows, on_chip(units), on_chip(mine), on_chip(other),
        *map(on_chip, tiles),
    )


def norm_call(tokens, gain):
    count, width = tokens.shape
    return pl.pallas_call(
        norm_kernel,
        out_shape=(
            pltpu.VMEM((width, count), jnp.bfloat16),
            pltpu.VMEM((count, 1), jnp.float32),
        ),
        in_specs=[VMEM, VMEM],
        out_specs=(VMEM, VMEM),
        compiler_params=pltpu.CompilerParams(vmem_limit_bytes=6 << 20),
    )(on_chip(tokens), gain)


def close_call(keep, came, tokens, gain, inverse):
    count, width = tokens.shape
    return pl.pallas_call(
        close_kernel,
        out_shape=jax.ShapeDtypeStruct((count, width), jnp.bfloat16),
        in_specs=[VMEM] * 5,
        out_specs=VMEM,
        scratch_shapes=[pltpu.VMEM((count, width), jnp.float32)],
        compiler_params=pltpu.CompilerParams(vmem_limit_bytes=6 << 20),
    )(
        on_chip(keep.reshape(width, count)), on_chip(came.reshape(width, count)), on_chip(tokens),
        gain, on_chip(inverse),
    )


def unit_kernel(high_ref, near_ref, far_ref, units_ref):
    near, far, high = near_ref[...], far_ref[...], high_ref[0]
    groups = near.shape[0] // GROUP
    for run in range(2):
        turned = jnp.where(high == run, near, far).T
        for g in range(groups):
            units_ref[run, g] = turned[:, g * GROUP : (g + 1) * GROUP]


def unit_call(high, near, far):
    columns, block = near.shape
    return pl.pallas_call(
        unit_kernel,
        out_shape=pltpu.VMEM((2, columns // GROUP, block, GROUP), jnp.float32),
        in_specs=[SMEM, VMEM, VMEM],
        out_specs=VMEM,
        compiler_params=pltpu.CompilerParams(vmem_limit_bytes=1 << 20),
    )(high, on_chip(near), on_chip(far))


def pack_tiles(tiles):
    lead = tiles.shape[:-1]
    split = tiles.reshape(*lead, 2, HALF, BLOCK)
    return jnp.moveaxis(split, -3, -2).reshape(*lead, HALF, 2 * BLOCK)


def on_device(tokens, norm_gain, penalty, weight_tiles, block_rows, block_slot):
    y, zl, x, zh, core = (lax.axis_index(name) for name in AXES)
    runs, slots, _ = weight_tiles.shape
    count, width = tokens.shape
    columns, per_column = block_rows.shape[0] // runs, block_rows.shape[1]

    def of_runs(table):
        paired = table.reshape(2, 2, columns * per_column)
        return lax.dynamic_index_in_dim(paired, core, 1, keepdims=False).reshape(-1)

    rows = of_runs(block_rows)
    places = of_runs(tile_places(block_slot, slots, y, zl, x, core))
    near = penalty.reshape(columns, BLOCK)
    own = pack_tiles(weight_tiles)
    tiles, (rows, places, near, high) = gather_tiles(own, core, (rows, places, near, zh.reshape(1)))
    gain = norm_gain.reshape(1, width)
    features, inverse = norm_call(tokens, gain)
    other = swap_cores(features)
    distant = lax.ppermute(near, "zh", [(0, 1), (1, 0)])
    units = unit_call(high, near, distant)
    blocks = (width // BLOCK, BLOCK, count)
    keep, send = sparse_call(
        columns, per_column, places, rows, units, features.reshape(blocks), other.reshape(blocks), tiles
    )
    came = swap_cores(send)
    return close_call(keep, came, tokens, gain, inverse)


def solution(mesh):
    fine = Mesh(mesh.devices.reshape(NY, NZ, NX, 2, 2), AXES)
    placed = (P(AXES, None), P(), P(("zh", "core")), P(None, ("y", "zl", "x"), None), P(), P())

    return jax.shard_map(
        on_device, mesh=fine, in_specs=placed, out_specs=P(AXES, None), check_vma=False
    )
```

```python
import jax
import jax.numpy as jnp
from jax import lax
from jax.experimental import pallas as pl
from jax.experimental.pallas import tpu as pltpu
from jax.sharding import Mesh
from jax.sharding import PartitionSpec as P

BLOCK = 64
HALF = BLOCK // 2
EPS = 1e-05
LANES = 128
GROUP = 28
ROWS = 32
NX, NY, NZ = 4, 4, 8
SIDE = 4
AXES = ("y", "zl", "x", "zh", "core")
SMEM = pl.BlockSpec(memory_space=pltpu.SMEM)
VMEM = pl.BlockSpec(memory_space=pltpu.VMEM)


def on_chip(x):
    return pltpu.with_memory_space_constraint(x, pltpu.VMEM)


def norm_kernel(tokens_ref, gain_ref, feat_ref, inverse_ref):
    x = tokens_ref[...].astype(jnp.float32)
    inverse = 1.0 / jnp.sqrt(jnp.mean(x * x, axis=1, keepdims=True) + EPS)
    inverse_ref[...] = inverse
    scaled = ((x * inverse) * gain_ref[...]).astype(jnp.bfloat16)
    for at in range(0, x.shape[1], LANES):
        feat_ref[at : at + LANES, :] = scaled[:, at : at + LANES].T


def invert_kernel(columns, per_column, tile_ref, row_ref, back_tile_ref, back_column_ref, count_ref):
    runs = 2
    blank = runs * SIDE * SIDE * NZ * 3
    spots = back_tile_ref.shape[0]

    def clear(i, carry):
        for j in range(4):
            back_tile_ref[4 * i + j] = blank
            back_column_ref[4 * i + j] = 0
        count_ref[i] = 0
        return carry

    lax.fori_loop(0, spots // 4, clear, 0)

    def note(column, carry):
        for k in range(per_column):
            at = column * per_column + k
            line = row_ref[at] + jnp.where(column < columns, 0, spots // 4 // runs)
            seen = count_ref[line]
            back_tile_ref[line * 4 + seen] = tile_ref[at]
            back_column_ref[line * 4 + seen] = column
            count_ref[line] = seen + 1
        return carry

    lax.fori_loop(0, runs * columns, note, 0)


def invert_call(columns, per_column, row_blocks, places, rows):
    spots = 2 * row_blocks * 4

    def body(*refs):
        invert_kernel(columns, per_column, *refs)

    return pl.pallas_call(
        body,
        out_shape=[jax.ShapeDtypeStruct((spots,), jnp.int32)] * 2,
        in_specs=[SMEM, SMEM],
        out_specs=[SMEM, SMEM],
        scratch_shapes=[pltpu.SMEM((spots // 4,), jnp.int32)],
        compiler_params=pltpu.CompilerParams(vmem_limit_bytes=1 << 20),
    )(places, rows)


def sparse_kernel(
    columns, per_column, tile_ref, row_ref, back_tile_ref, back_column_ref, unit_ref, mine_ref,
    other_ref, *refs
):
    parts, (keep_ref, send_ref, grad_ref, w_ref, sems) = refs[:8], refs[8:]
    row_blocks, _, count = mine_ref.shape
    size = parts[0].shape[0]
    copies = []
    for i, source in enumerate(parts):
        run, at = i // SIDE, i % SIDE
        target = w_ref.at[pl.ds(i * size, size)]
        copies.append(pltpu.make_async_copy(source, target, sems.at[run, at]))
    for copy in copies:
        copy.start()
    w_ref[len(parts) * size] = jnp.zeros(w_ref.shape[1:], w_ref.dtype)

    def forward(g, j):
        at = (g * GROUP + j) * per_column
        rows = [row_ref[at + k] for k in range(per_column)]
        tiles = [w_ref[tile_ref[at + k]] for k in range(per_column)]
        turned = jnp.concatenate(tiles, axis=0).T
        lhs = jnp.concatenate([turned[:BLOCK], turned[BLOCK:]], axis=1)
        mine = [mine_ref[r] for r in rows]
        other = [other_ref[r] for r in rows]
        rhs = jnp.concatenate(
            [
                jnp.concatenate([p[:HALF] for p in side] + [p[HALF:] for p in side], axis=0)
                for side in (mine, other)
            ],
            axis=1,
        )
        preact = jnp.dot(lhs, rhs, preferred_element_type=jnp.float32)
        gating = jax.nn.sigmoid(preact)
        grad_act = unit_ref[g][:, j : j + 1] * (preact * gating)
        grad_pre = grad_act * (gating * (1.0 + preact * (1.0 - gating)))
        grad_ref[g * GROUP + j] = grad_pre.astype(jnp.bfloat16)

    def ahead(g, carry):
        for j in range(GROUP):
            forward(g, j)
        return carry

    left = lax.broadcasted_iota(jnp.int32, (HALF, 2 * BLOCK), 1) < BLOCK

    def backward(row):
        total = None
        for run in range(2):
            at = (run * row_blocks + row) * 4
            upper, lower = [], []
            for k in range(0, 4, 2):
                first, second = w_ref[back_tile_ref[at + k]], w_ref[back_tile_ref[at + k + 1]]
                upper.append(jnp.where(left, first, pltpu.roll(second, BLOCK, 1)))
                lower.append(jnp.where(left, pltpu.roll(first, BLOCK, 1), second))
            lhs = jnp.concatenate(
                [jnp.concatenate(upper, axis=1), jnp.concatenate(lower, axis=1)], axis=0
            )
            rhs = jnp.concatenate([grad_ref[back_column_ref[at + k]] for k in range(4)], axis=0)
            part = jnp.dot(lhs, rhs, preferred_element_type=jnp.float32)
            total = part if total is None else total + part
        keep_ref[row] = total[:, :count]
        send_ref[row] = total[:, count:].astype(jnp.bfloat16)

    def back(g, carry):
        for j in range(ROWS):
            backward(g * ROWS + j)
        return carry

    groups = columns // GROUP
    for run in range(2):
        for copy in copies[run * SIDE : (run + 1) * SIDE]:
            copy.wait()
        lax.fori_loop(run * groups, (run + 1) * groups, ahead, 0)
    lax.fori_loop(0, row_blocks // ROWS, back, 0)


def close_kernel(keep_ref, came_ref, tokens_ref, gain_ref, inverse_ref, out_ref, grad_ref):
    inverse = inverse_ref[...]
    width = tokens_ref.shape[1]
    total = jnp.zeros((tokens_ref.shape[0], LANES), jnp.float32)
    for at in range(0, width, LANES):
        span = slice(at, at + LANES)
        grad = (keep_ref[span, :] + came_ref[span, :].astype(jnp.float32)).T
        grad = grad * gain_ref[:, span]
        grad_ref[:, span] = grad
        total += grad * (tokens_ref[:, span].astype(jnp.float32) * inverse)
    mixing = jnp.sum(total, axis=1, keepdims=True) * (1.0 / width)
    for at in range(0, width, LANES):
        span = slice(at, at + LANES)
        normed = tokens_ref[:, span].astype(jnp.float32) * inverse
        out_ref[:, span] = ((grad_ref[:, span] - normed * mixing) * inverse).astype(jnp.bfloat16)


def along_z(v, step):
    size = 2 * NZ
    pairs = []
    for z in range(size):
        for core in range(2):
            to = (z + (step if core == 0 else -step)) % size
            pairs.append([((at % NZ) * 2 + at // NZ) * 2 + core for at in (z, to)])
    return lax.ppermute(v, ("zl", "zh", "core"), pairs)


def along_side(v, step, leg):
    pairs = []
    for y in range(NY):
        for x in range(NX):
            for core in range(2):
                to_y, to_x = (y, (x + step) % NX) if core == leg else ((y + step) % NY, x)
                pairs.append(((y * NX + x) * 2 + core, (to_y * NX + to_x) * 2 + core))
    return lax.ppermute(v, ("y", "x", "core"), pairs)


def swap_cores(v):
    return lax.ppermute(v, "core", [(0, 1), (1, 0)])


def join_kernel(line_ref, ahead_ref, across_ref, back_ref, *plane_refs):
    size = line_ref.shape[1]
    for run, plane_ref in enumerate(plane_refs):
        for i, ref in enumerate((line_ref, ahead_ref, across_ref, back_ref)):
            plane_ref[i * size : (i + 1) * size] = ref[run]


def join(*parts):
    runs, size, *tile = parts[0].shape
    return pl.pallas_call(
        join_kernel,
        out_shape=[pltpu.VMEM((SIDE * size, *tile), parts[0].dtype)] * runs,
        in_specs=[VMEM] * len(parts),
        out_specs=[VMEM] * runs,
        compiler_params=pltpu.CompilerParams(vmem_limit_bytes=1 << 20),
    )(*map(on_chip, parts))


def of_core(table, core):
    paired = table.reshape(*table.shape[:-4], 2, 2, *table.shape[-3:])
    return lax.dynamic_index_in_dim(paired, core, paired.ndim - 4, keepdims=False)


def gather_tiles(own, core, early):
    _, slots = own.shape[:2]
    mine = of_core(own, core)
    far = along_z(own, 3)
    opposite = along_z(mine, 4)
    middle = along_z(own, 2)
    near = along_z(own, 1)
    near, middle, far, early = lax.optimization_barrier((near, middle, far, early))
    side = jnp.stack([near, middle, far])
    theirs = swap_cores(of_core(side, 1 - core))
    line = jnp.concatenate([mine[None], of_core(side, core), opposite[None], theirs], axis=0)
    line = line.transpose(1, 0, 2, 3, 4).reshape(2, NZ * slots, HALF, 2 * BLOCK)
    across, back, ahead = along_side(line, 2, 0), along_side(line, 1, 0), along_side(line, -1, 0)
    planes = join(line, ahead, across, back)
    back_0, ahead_1 = along_side(planes[0], 1, 1), along_side(planes[1], -1, 1)
    back_1, ahead_0 = along_side(planes[1], 1, 1), along_side(planes[0], -1, 1)
    across_0, across_1 = along_side(back_0, 1, 1), along_side(ahead_1, -1, 1)
    pieces = [planes[0], ahead_0, across_0, back_0, planes[1], ahead_1, across_1, back_1]
    return pieces, early


def tile_places(block_slot, slots, y, zl, x, core):
    owner, place = block_slot // slots, block_slot % slots
    step_x = (owner % NX - x) % NX
    step_z = ((owner // NX) % NZ - zl) * (2 * core - 1) % NZ
    step_z = jnp.where(step_z > NZ // 2, 3 * NZ // 2 - step_z, step_z)
    step_y = (owner // (NX * NZ) - y) % NY
    first = jnp.where(core == 0, step_x, step_y)
    second = jnp.where(core == 0, step_y, step_x)
    return ((second * SIDE + first) * NZ + step_z) * slots + place


def sparse_call(columns, per_column, places, rows, back_places, back_columns, units, mine, other, tiles):
    row_blocks, _, count = mine.shape

    def body(*refs):
        sparse_kernel(columns, per_column, *refs)

    return pl.pallas_call(
        body,
        out_shape=(
            pltpu.VMEM((row_blocks, BLOCK, count), jnp.float32),
            pltpu.VMEM((row_blocks, BLOCK, count), jnp.bfloat16),
        ),
        in_specs=[SMEM] * 4 + [VMEM] * 11,
        out_specs=(VMEM, VMEM),
        scratch_shapes=[
            pltpu.VMEM((2 * columns, BLOCK, 2 * count), jnp.bfloat16),
            pltpu.VMEM((len(tiles) * tiles[0].shape[0] + 1, HALF, 2 * BLOCK), jnp.bfloat16),
            pltpu.SemaphoreType.DMA((2, 4)),
        ],
        compiler_params=pltpu.CompilerParams(vmem_limit_bytes=14 << 20),
    )(
        places, rows, back_places, back_columns, on_chip(units), on_chip(mine), on_chip(other),
        *map(on_chip, tiles),
    )


def norm_call(tokens, gain):
    count, width = tokens.shape
    return pl.pallas_call(
        norm_kernel,
        out_shape=(
            pltpu.VMEM((width, count), jnp.bfloat16),
            pltpu.VMEM((count, 1), jnp.float32),
        ),
        in_specs=[VMEM, VMEM],
        out_specs=(VMEM, VMEM),
        compiler_params=pltpu.CompilerParams(vmem_limit_bytes=6 << 20),
    )(on_chip(tokens), gain)


def close_call(keep, came, tokens, gain, inverse):
    count, width = tokens.shape
    return pl.pallas_call(
        close_kernel,
        out_shape=jax.ShapeDtypeStruct((count, width), jnp.bfloat16),
        in_specs=[VMEM] * 5,
        out_specs=VMEM,
        scratch_shapes=[pltpu.VMEM((count, width), jnp.float32)],
        compiler_params=pltpu.CompilerParams(vmem_limit_bytes=6 << 20),
    )(
        on_chip(keep.reshape(width, count)), on_chip(came.reshape(width, count)), on_chip(tokens),
        gain, on_chip(inverse),
    )


def unit_kernel(high_ref, near_ref, far_ref, units_ref):
    near, far, high = near_ref[...], far_ref[...], high_ref[0]
    groups = near.shape[0] // GROUP
    for run in range(2):
        turned = jnp.where(high == run, near, far).T
        for g in range(groups):
            units_ref[run * groups + g] = turned[:, g * GROUP : (g + 1) * GROUP]


def unit_call(high, near, far):
    columns, block = near.shape
    return pl.pallas_call(
        unit_kernel,
        out_shape=pltpu.VMEM((2 * columns // GROUP, block, GROUP), jnp.float32),
        in_specs=[SMEM, VMEM, VMEM],
        out_specs=VMEM,
        compiler_params=pltpu.CompilerParams(vmem_limit_bytes=1 << 20),
    )(high, on_chip(near), on_chip(far))


def pack_tiles(tiles):
    lead = tiles.shape[:-1]
    split = tiles.reshape(*lead, 2, HALF, BLOCK)
    return jnp.moveaxis(split, -3, -2).reshape(*lead, HALF, 2 * BLOCK)


def on_device(tokens, norm_gain, penalty, weight_tiles, block_rows, block_slot):
    y, zl, x, zh, core = (lax.axis_index(name) for name in AXES)
    runs, slots, _ = weight_tiles.shape
    count, width = tokens.shape
    columns, per_column = block_rows.shape[0] // runs, block_rows.shape[1]

    def of_runs(table):
        paired = table.reshape(2, 2, columns * per_column)
        return lax.dynamic_index_in_dim(paired, core, 1, keepdims=False).reshape(-1)

    rows = of_runs(block_rows)
    places = tile_places(block_slot, slots, y, zl, x, core).reshape(runs, columns * per_column)
    second = jnp.arange(runs)[:, None] // 2 * (NX * NY * NZ * slots)
    places = of_runs(places + second)
    near = penalty.reshape(columns, BLOCK)
    own = pack_tiles(weight_tiles)
    tiles, (rows, places, near, high) = gather_tiles(own, core, (rows, places, near, zh.reshape(1)))
    gain = norm_gain.reshape(1, width)
    features, inverse = norm_call(tokens, gain)
    other = swap_cores(features)
    distant = lax.ppermute(near, "zh", [(0, 1), (1, 0)])
    units = unit_call(high, near, distant)
    blocks = (width // BLOCK, BLOCK, count)
    back = invert_call(columns, per_column, width // BLOCK, places, rows)
    keep, send = sparse_call(
        columns, per_column, places, rows, *back, units, features.reshape(blocks), other.reshape(blocks), tiles
    )
    came = swap_cores(send)
    return close_call(keep, came, tokens, gain, inverse)


def solution(mesh):
    fine = Mesh(mesh.devices.reshape(NY, NZ, NX, 2, 2), AXES)
    placed = (P(AXES, None), P(), P(("zh", "core")), P(None, ("y", "zl", "x"), None), P(), P())

    return jax.shard_map(on_device, mesh=fine, in_specs=placed, out_specs=P(AXES, None), check_vma=False)
```

```python
import jax
import jax.numpy as jnp
from jax import lax
from jax.experimental import pallas as pl
from jax.experimental.pallas import tpu as pltpu
from jax.sharding import Mesh
from jax.sharding import PartitionSpec as P

BLOCK = 64
HALF = BLOCK // 2
EPS = 1e-05
LANES = 128
GROUP = 28
ROWS = 32
NX, NY, NZ = 4, 4, 8
SIDE = 4
AXES = ("y", "zl", "x", "zh", "core")
SMEM = pl.BlockSpec(memory_space=pltpu.SMEM)
VMEM = pl.BlockSpec(memory_space=pltpu.VMEM)


def on_chip(x):
    return pltpu.with_memory_space_constraint(x, pltpu.VMEM)


def norm_kernel(tokens_ref, gain_ref, feat_ref, inverse_ref):
    x = tokens_ref[...].astype(jnp.float32)
    inverse = 1.0 / jnp.sqrt(jnp.mean(x * x, axis=1, keepdims=True) + EPS)
    inverse_ref[...] = inverse
    scaled = ((x * inverse) * gain_ref[...]).astype(jnp.bfloat16)
    for at in range(0, x.shape[1], LANES):
        feat_ref[at : at + LANES, :] = scaled[:, at : at + LANES].T


def invert_kernel(columns, per_column, tile_ref, row_ref, back_tile_ref, back_column_ref, count_ref):
    runs = 2
    blank = runs * SIDE * SIDE * NZ * 3
    spots = back_tile_ref.shape[0]

    def clear(i, carry):
        for j in range(4):
            back_tile_ref[4 * i + j] = blank
            back_column_ref[4 * i + j] = 0
        count_ref[i] = 0
        return carry

    lax.fori_loop(0, spots // 4, clear, 0)

    def note(column, carry):
        for k in range(per_column):
            at = column * per_column + k
            line = row_ref[at] + jnp.where(column < columns, 0, spots // 4 // runs)
            seen = count_ref[line]
            back_tile_ref[line * 4 + seen] = tile_ref[at]
            back_column_ref[line * 4 + seen] = column
            count_ref[line] = seen + 1
        return carry

    lax.fori_loop(0, runs * columns, note, 0)


def invert_call(columns, per_column, row_blocks, places, rows):
    spots = 2 * row_blocks * 4

    def body(*refs):
        invert_kernel(columns, per_column, *refs)

    return pl.pallas_call(
        body,
        out_shape=[jax.ShapeDtypeStruct((spots,), jnp.int32)] * 2,
        in_specs=[SMEM, SMEM],
        out_specs=[SMEM, SMEM],
        scratch_shapes=[pltpu.SMEM((spots // 4,), jnp.int32)],
        compiler_params=pltpu.CompilerParams(vmem_limit_bytes=1 << 20),
    )(places, rows)


def fill_kernel(pieces, *refs):
    parts, w_ref = refs[:-1], refs[-1]
    size = parts[0].shape[0]
    for piece, ref in zip(pieces, parts):
        w_ref[piece * size : (piece + 1) * size] = ref[...]
    w_ref[w_ref.shape[0] - 1] = jnp.zeros(w_ref.shape[1:], w_ref.dtype)


def fill_call(pieces, arrays):
    def body(*refs):
        fill_kernel(pieces, *refs)

    size, *tile = arrays[0].shape
    return pl.pallas_call(
        body,
        out_shape=pltpu.VMEM((2 * SIDE * size + 1, *tile), arrays[0].dtype),
        in_specs=[VMEM] * len(arrays),
        out_specs=VMEM,
        compiler_params=pltpu.CompilerParams(vmem_limit_bytes=1 << 20),
    )(*map(on_chip, arrays))


def back_row(tile_ref, column_ref, w_ref, grad_ref, row_blocks, row, lanes):
    left = lax.broadcasted_iota(jnp.int32, (HALF, 2 * BLOCK), 1) < BLOCK
    total = None
    for run in range(2):
        at = (run * row_blocks + row) * 4
        upper, lower = [], []
        for k in range(0, 4, 2):
            first, second = w_ref[tile_ref[at + k]], w_ref[tile_ref[at + k + 1]]
            upper.append(jnp.where(left, first, pltpu.roll(second, BLOCK, 1)))
            lower.append(jnp.where(left, pltpu.roll(first, BLOCK, 1), second))
        lhs = jnp.concatenate(
            [jnp.concatenate(upper, axis=1), jnp.concatenate(lower, axis=1)], axis=0
        )
        rhs = jnp.concatenate([grad_ref[column_ref[at + k], :, lanes] for k in range(4)], axis=0)
        part = jnp.dot(lhs, rhs, preferred_element_type=jnp.float32)
        total = part if total is None else total + part
    return total


def keep_kernel(tile_ref, column_ref, w_ref, grad_ref, keep_ref):
    row_blocks, _, count = keep_ref.shape

    def back(g, carry):
        for j in range(ROWS):
            row = g * ROWS + j
            keep_ref[row] = back_row(
                tile_ref, column_ref, w_ref, grad_ref, row_blocks, row, slice(0, count)
            )
        return carry

    lax.fori_loop(0, row_blocks // ROWS, back, 0)


def sparse_kernel(
    columns, per_column, tile_ref, row_ref, back_tile_ref, back_column_ref, unit_ref, mine_ref,
    other_ref, old_ref, first_ref, second_ref, w_ref, grad_ref, send_ref
):
    row_blocks, _, count = mine_ref.shape
    size = first_ref.shape[0]
    del old_ref
    for run, ref in enumerate((first_ref, second_ref)):
        at = (run * SIDE + 2) * size
        w_ref[at : at + size] = ref[...]

    def forward(g, j):
        at = (g * GROUP + j) * per_column
        rows = [row_ref[at + k] for k in range(per_column)]
        tiles = [w_ref[tile_ref[at + k]] for k in range(per_column)]
        turned = jnp.concatenate(tiles, axis=0).T
        lhs = jnp.concatenate([turned[:BLOCK], turned[BLOCK:]], axis=1)
        mine = [mine_ref[r] for r in rows]
        other = [other_ref[r] for r in rows]
        rhs = jnp.concatenate(
            [
                jnp.concatenate([p[:HALF] for p in side] + [p[HALF:] for p in side], axis=0)
                for side in (mine, other)
            ],
            axis=1,
        )
        preact = jnp.dot(lhs, rhs, preferred_element_type=jnp.float32)
        gating = jax.nn.sigmoid(preact)
        grad_act = unit_ref[g][:, j : j + 1] * (preact * gating)
        grad_pre = grad_act * (gating * (1.0 + preact * (1.0 - gating)))
        grad_ref[g * GROUP + j] = grad_pre.astype(jnp.bfloat16)

    def ahead(g, carry):
        for j in range(GROUP):
            forward(g, j)
        return carry

    def back(g, carry):
        for j in range(ROWS):
            row = g * ROWS + j
            send_ref[row] = back_row(
                back_tile_ref, back_column_ref, w_ref, grad_ref, row_blocks, row, slice(count, None)
            ).astype(jnp.bfloat16)
        return carry

    lax.fori_loop(0, 2 * columns // GROUP, ahead, 0)
    lax.fori_loop(0, row_blocks // ROWS, back, 0)


def close_kernel(keep_ref, came_ref, tokens_ref, gain_ref, inverse_ref, out_ref, grad_ref):
    inverse = inverse_ref[...]
    width = tokens_ref.shape[1]
    total = jnp.zeros((tokens_ref.shape[0], LANES), jnp.float32)
    for at in range(0, width, LANES):
        span = slice(at, at + LANES)
        grad = (keep_ref[span, :] + came_ref[span, :].astype(jnp.float32)).T
        grad = grad * gain_ref[:, span]
        grad_ref[:, span] = grad
        total += grad * (tokens_ref[:, span].astype(jnp.float32) * inverse)
    mixing = jnp.sum(total, axis=1, keepdims=True) * (1.0 / width)
    for at in range(0, width, LANES):
        span = slice(at, at + LANES)
        normed = tokens_ref[:, span].astype(jnp.float32) * inverse
        out_ref[:, span] = ((grad_ref[:, span] - normed * mixing) * inverse).astype(jnp.bfloat16)


def along_z(v, step):
    size = 2 * NZ
    pairs = []
    for z in range(size):
        for core in range(2):
            to = (z + (step if core == 0 else -step)) % size
            pairs.append([((at % NZ) * 2 + at // NZ) * 2 + core for at in (z, to)])
    return lax.ppermute(v, ("zl", "zh", "core"), pairs)


def along_side(v, step, leg):
    pairs = []
    for y in range(NY):
        for x in range(NX):
            for core in range(2):
                to_y, to_x = (y, (x + step) % NX) if core == leg else ((y + step) % NY, x)
                pairs.append(((y * NX + x) * 2 + core, (to_y * NX + to_x) * 2 + core))
    return lax.ppermute(v, ("y", "x", "core"), pairs)


def swap_cores(v):
    return lax.ppermute(v, "core", [(0, 1), (1, 0)])


def join_kernel(line_ref, ahead_ref, across_ref, back_ref, *plane_refs):
    size = line_ref.shape[1]
    for run, plane_ref in enumerate(plane_refs):
        for i, ref in enumerate((line_ref, ahead_ref, across_ref, back_ref)):
            plane_ref[i * size : (i + 1) * size] = ref[run]


def join(*parts):
    runs, size, *tile = parts[0].shape
    return pl.pallas_call(
        join_kernel,
        out_shape=[pltpu.VMEM((SIDE * size, *tile), parts[0].dtype)] * runs,
        in_specs=[VMEM] * len(parts),
        out_specs=[VMEM] * runs,
        compiler_params=pltpu.CompilerParams(vmem_limit_bytes=1 << 20),
    )(*map(on_chip, parts))


def of_core(table, core):
    paired = table.reshape(*table.shape[:-4], 2, 2, *table.shape[-3:])
    return lax.dynamic_index_in_dim(paired, core, paired.ndim - 4, keepdims=False)


def gather_tiles(own, core, early):
    _, slots = own.shape[:2]
    mine = of_core(own, core)
    far = along_z(own, 3)
    middle = along_z(own, 2)
    near = along_z(own, 1)
    opposite = along_z(of_core(middle, core), 2)
    near, middle, far, early = lax.optimization_barrier((near, middle, far, early))
    side = jnp.stack([near, middle, far])
    theirs = swap_cores(of_core(side, 1 - core))
    line = jnp.concatenate([mine[None], of_core(side, core), opposite[None], theirs], axis=0)
    line = line.transpose(1, 0, 2, 3, 4).reshape(2, NZ * slots, HALF, 2 * BLOCK)
    across, back, ahead = along_side(line, 2, 0), along_side(line, 1, 0), along_side(line, -1, 0)
    planes = join(line, ahead, across, back)
    back_0, ahead_1 = along_side(planes[0], 1, 1), along_side(planes[1], -1, 1)
    back_1, ahead_0 = along_side(planes[1], 1, 1), along_side(planes[0], -1, 1)
    across_0, across_1 = along_side(back_0, 1, 1), along_side(ahead_1, -1, 1)
    pieces = [planes[0], ahead_0, across_0, back_0, planes[1], ahead_1, across_1, back_1]
    return pieces, early


def tile_places(block_slot, slots, y, zl, x, core):
    owner, place = block_slot // slots, block_slot % slots
    step_x = (owner % NX - x) % NX
    step_z = ((owner // NX) % NZ - zl) * (2 * core - 1) % NZ
    step_z = jnp.where(step_z > NZ // 2, 3 * NZ // 2 - step_z, step_z)
    step_y = (owner // (NX * NZ) - y) % NY
    first = jnp.where(core == 0, step_x, step_y)
    second = jnp.where(core == 0, step_y, step_x)
    return ((second * SIDE + first) * NZ + step_z) * slots + place


def sparse_call(columns, per_column, places, rows, back_places, back_columns, units, mine, other, tiles):
    row_blocks, _, count = mine.shape
    late = (2, SIDE + 2)
    early = [i for i in range(len(tiles)) if i not in late]
    filled = fill_call(early, [tiles[i] for i in early])

    def body(*refs):
        sparse_kernel(columns, per_column, *refs)

    full, grads, send = pl.pallas_call(
        body,
        out_shape=(
            pltpu.VMEM(filled.shape, filled.dtype),
            pltpu.VMEM((2 * columns, BLOCK, 2 * count), jnp.bfloat16),
            pltpu.VMEM((row_blocks, BLOCK, count), jnp.bfloat16),
        ),
        in_specs=[SMEM] * 4 + [VMEM] * 6,
        out_specs=(VMEM, VMEM, VMEM),
        input_output_aliases={7: 0},
        compiler_params=pltpu.CompilerParams(vmem_limit_bytes=3 << 20),
    )(
        places, rows, back_places, back_columns, on_chip(units), on_chip(mine), on_chip(other),
        on_chip(filled), *(on_chip(tiles[i]) for i in late),
    )
    came = swap_cores(send)
    keep = pl.pallas_call(
        keep_kernel,
        out_shape=pltpu.VMEM((row_blocks, BLOCK, count), jnp.float32),
        in_specs=[SMEM] * 2 + [VMEM] * 2,
        out_specs=VMEM,
        compiler_params=pltpu.CompilerParams(vmem_limit_bytes=3 << 20),
    )(back_places, back_columns, on_chip(full), on_chip(grads))
    return keep, came


def norm_call(tokens, gain):
    count, width = tokens.shape
    return pl.pallas_call(
        norm_kernel,
        out_shape=(
            pltpu.VMEM((width, count), jnp.bfloat16),
            pltpu.VMEM((count, 1), jnp.float32),
        ),
        in_specs=[VMEM, VMEM],
        out_specs=(VMEM, VMEM),
        compiler_params=pltpu.CompilerParams(vmem_limit_bytes=6 << 20),
    )(on_chip(tokens), gain)


def close_call(keep, came, tokens, gain, inverse):
    count, width = tokens.shape
    return pl.pallas_call(
        close_kernel,
        out_shape=jax.ShapeDtypeStruct((count, width), jnp.bfloat16),
        in_specs=[VMEM] * 5,
        out_specs=VMEM,
        scratch_shapes=[pltpu.VMEM((count, width), jnp.float32)],
        compiler_params=pltpu.CompilerParams(vmem_limit_bytes=6 << 20),
    )(
        on_chip(keep.reshape(width, count)), on_chip(came.reshape(width, count)), on_chip(tokens),
        gain, on_chip(inverse),
    )


def unit_kernel(high_ref, near_ref, far_ref, units_ref):
    near, far, high = near_ref[...], far_ref[...], high_ref[0]
    groups = near.shape[0] // GROUP
    for run in range(2):
        turned = jnp.where(high == run, near, far).T
        for g in range(groups):
            units_ref[run * groups + g] = turned[:, g * GROUP : (g + 1) * GROUP]


def unit_call(high, near, far):
    columns, block = near.shape
    return pl.pallas_call(
        unit_kernel,
        out_shape=pltpu.VMEM((2 * columns // GROUP, block, GROUP), jnp.float32),
        in_specs=[SMEM, VMEM, VMEM],
        out_specs=VMEM,
        compiler_params=pltpu.CompilerParams(vmem_limit_bytes=1 << 20),
    )(high, on_chip(near), on_chip(far))


def pack_tiles(tiles):
    lead = tiles.shape[:-1]
    split = tiles.reshape(*lead, 2, HALF, BLOCK)
    return jnp.moveaxis(split, -3, -2).reshape(*lead, HALF, 2 * BLOCK)


def on_device(tokens, norm_gain, penalty, weight_tiles, block_rows, block_slot):
    y, zl, x, zh, core = (lax.axis_index(name) for name in AXES)
    runs, slots, _ = weight_tiles.shape
    count, width = tokens.shape
    columns, per_column = block_rows.shape[0] // runs, block_rows.shape[1]

    def of_runs(table):
        paired = table.reshape(2, 2, columns * per_column)
        return lax.dynamic_index_in_dim(paired, core, 1, keepdims=False).reshape(-1)

    rows = of_runs(block_rows)
    places = tile_places(block_slot, slots, y, zl, x, core).reshape(runs, columns * per_column)
    second = jnp.arange(runs)[:, None] // 2 * (NX * NY * NZ * slots)
    places = of_runs(places + second)
    near = penalty.reshape(columns, BLOCK)
    own = pack_tiles(weight_tiles)
    tiles, (rows, places, near, high) = gather_tiles(own, core, (rows, places, near, zh.reshape(1)))
    gain = norm_gain.reshape(1, width)
    features, inverse = norm_call(tokens, gain)
    other = swap_cores(features)
    distant = lax.ppermute(near, "zh", [(0, 1), (1, 0)])
    units = unit_call(high, near, distant)
    blocks = (width // BLOCK, BLOCK, count)
    back = invert_call(columns, per_column, width // BLOCK, places, rows)
    keep, came = sparse_call(
        columns, per_column, places, rows, *back, units, features.reshape(blocks), other.reshape(blocks), tiles
    )
    return close_call(keep, came, tokens, gain, inverse)


def solution(mesh):
    fine = Mesh(mesh.devices.reshape(NY, NZ, NX, 2, 2), AXES)
    placed = (P(AXES, None), P(), P(("zh", "core")), P(None, ("y", "zl", "x"), None), P(), P())

    return jax.shard_map(on_device, mesh=fine, in_specs=placed, out_specs=P(AXES, None), check_vma=False)
```

```python
import jax
import jax.numpy as jnp
from jax import lax
from jax.experimental import pallas as pl
from jax.experimental.pallas import tpu as pltpu
from jax.sharding import Mesh
from jax.sharding import PartitionSpec as P

BLOCK = 64
HALF = BLOCK // 2
EPS = 1e-05
LANES = 128
GROUP = 28
ROWS = 32
NX, NY, NZ = 4, 4, 8
SIDE = 4
AXES = ("y", "zl", "x", "zh", "core")
SMEM = pl.BlockSpec(memory_space=pltpu.SMEM)
VMEM = pl.BlockSpec(memory_space=pltpu.VMEM)


def on_chip(x):
    return pltpu.with_memory_space_constraint(x, pltpu.VMEM)


def norm_kernel(tokens_ref, gain_ref, feat_ref, inverse_ref):
    x = tokens_ref[...].astype(jnp.float32)
    inverse = 1.0 / jnp.sqrt(jnp.mean(x * x, axis=1, keepdims=True) + EPS)
    inverse_ref[...] = inverse
    scaled = ((x * inverse) * gain_ref[...]).astype(jnp.bfloat16)
    for at in range(0, x.shape[1], LANES):
        feat_ref[at : at + LANES, :] = scaled[:, at : at + LANES].T


def invert_kernel(columns, per_column, tile_ref, row_ref, back_tile_ref, back_column_ref, count_ref):
    runs = 2
    blank = runs * SIDE * SIDE * NZ * 3
    spots = back_tile_ref.shape[0]

    def clear(i, carry):
        for j in range(4):
            back_tile_ref[4 * i + j] = blank
            back_column_ref[4 * i + j] = 0
        count_ref[i] = 0
        return carry

    lax.fori_loop(0, spots // 4, clear, 0)

    def note(column, carry):
        for k in range(per_column):
            at = column * per_column + k
            line = row_ref[at] + jnp.where(column < columns, 0, spots // 4 // runs)
            seen = count_ref[line]
            back_tile_ref[line * 4 + seen] = tile_ref[at]
            back_column_ref[line * 4 + seen] = column
            count_ref[line] = seen + 1
        return carry

    lax.fori_loop(0, runs * columns, note, 0)


def invert_call(columns, per_column, row_blocks, places, rows):
    spots = 2 * row_blocks * 4

    def body(*refs):
        invert_kernel(columns, per_column, *refs)

    return pl.pallas_call(
        body,
        out_shape=[jax.ShapeDtypeStruct((spots,), jnp.int32)] * 2,
        in_specs=[SMEM, SMEM],
        out_specs=[SMEM, SMEM],
        scratch_shapes=[pltpu.SMEM((spots // 4,), jnp.int32)],
        compiler_params=pltpu.CompilerParams(vmem_limit_bytes=1 << 20),
    )(places, rows)


def fill_kernel(pieces, *refs):
    parts, w_ref = refs[:-1], refs[-1]
    size = parts[0].shape[0]
    for piece, ref in zip(pieces, parts):
        w_ref[piece * size : (piece + 1) * size] = ref[...]
    w_ref[w_ref.shape[0] - 1] = jnp.zeros(w_ref.shape[1:], w_ref.dtype)


def fill_call(pieces, arrays):
    def body(*refs):
        fill_kernel(pieces, *refs)

    size, *tile = arrays[0].shape
    return pl.pallas_call(
        body,
        out_shape=pltpu.VMEM((2 * SIDE * size + 1, *tile), arrays[0].dtype),
        in_specs=[VMEM] * len(arrays),
        out_specs=VMEM,
        compiler_params=pltpu.CompilerParams(vmem_limit_bytes=1 << 20),
    )(*map(on_chip, arrays))


def back_row(tile_ref, column_ref, w_ref, grad_ref, row_blocks, row, lanes):
    left = lax.broadcasted_iota(jnp.int32, (HALF, 2 * BLOCK), 1) < BLOCK
    total = None
    for run in range(2):
        at = (run * row_blocks + row) * 4
        upper, lower = [], []
        for k in range(0, 4, 2):
            first, second = w_ref[tile_ref[at + k]], w_ref[tile_ref[at + k + 1]]
            upper.append(jnp.where(left, first, pltpu.roll(second, BLOCK, 1)))
            lower.append(jnp.where(left, pltpu.roll(first, BLOCK, 1), second))
        lhs = jnp.concatenate(
            [jnp.concatenate(upper, axis=1), jnp.concatenate(lower, axis=1)], axis=0
        )
        rhs = jnp.concatenate([grad_ref[column_ref[at + k], :, lanes] for k in range(4)], axis=0)
        part = jnp.dot(lhs, rhs, preferred_element_type=jnp.float32)
        total = part if total is None else total + part
    return total


def keep_kernel(tile_ref, column_ref, w_ref, grad_ref, keep_ref):
    row_blocks, _, count = keep_ref.shape

    def back(g, carry):
        for j in range(ROWS):
            row = g * ROWS + j
            keep_ref[row] = back_row(
                tile_ref, column_ref, w_ref, grad_ref, row_blocks, row, slice(0, count)
            )
        return carry

    lax.fori_loop(0, row_blocks // ROWS, back, 0)


def sparse_kernel(
    columns, per_column, tile_ref, row_ref, back_tile_ref, back_column_ref, unit_ref, mine_ref,
    other_ref, old_ref, first_ref, second_ref, w_ref, grad_ref, send_ref
):
    row_blocks, _, count = mine_ref.shape
    size = first_ref.shape[0]
    del old_ref
    for run, ref in enumerate((first_ref, second_ref)):
        at = (run * SIDE + 2) * size
        w_ref[at : at + size] = ref[...]

    def forward(g, j):
        at = (g * GROUP + j) * per_column
        rows = [row_ref[at + k] for k in range(per_column)]
        tiles = [w_ref[tile_ref[at + k]] for k in range(per_column)]
        turned = jnp.concatenate(tiles, axis=0).T
        lhs = jnp.concatenate([turned[:BLOCK], turned[BLOCK:]], axis=1)
        mine = [mine_ref[r] for r in rows]
        other = [other_ref[r] for r in rows]
        rhs = jnp.concatenate(
            [
                jnp.concatenate([p[:HALF] for p in side] + [p[HALF:] for p in side], axis=0)
                for side in (mine, other)
            ],
            axis=1,
        )
        preact = jnp.dot(lhs, rhs, preferred_element_type=jnp.float32)
        gating = jax.nn.sigmoid(preact)
        grad_act = unit_ref[g][:, j : j + 1] * (preact * gating)
        grad_pre = grad_act * (gating * (1.0 + preact * (1.0 - gating)))
        grad_ref[g * GROUP + j] = grad_pre.astype(jnp.bfloat16)

    def ahead(g, carry):
        for j in range(GROUP):
            forward(g, j)
        return carry

    def back(g, carry):
        for j in range(ROWS):
            row = g * ROWS + j
            send_ref[row] = back_row(
                back_tile_ref, back_column_ref, w_ref, grad_ref, row_blocks, row, slice(count, None)
            ).astype(jnp.bfloat16)
        return carry

    lax.fori_loop(0, 2 * columns // GROUP, ahead, 0)
    lax.fori_loop(0, row_blocks // ROWS, back, 0)


def close_kernel(keep_ref, came_ref, tokens_ref, gain_ref, inverse_ref, out_ref, grad_ref):
    inverse = inverse_ref[...]
    width = tokens_ref.shape[1]
    total = jnp.zeros((tokens_ref.shape[0], LANES), jnp.float32)
    for at in range(0, width, LANES):
        span = slice(at, at + LANES)
        grad = (keep_ref[span, :] + came_ref[span, :].astype(jnp.float32)).T
        grad = grad * gain_ref[:, span]
        grad_ref[:, span] = grad
        total += grad * (tokens_ref[:, span].astype(jnp.float32) * inverse)
    mixing = jnp.sum(total, axis=1, keepdims=True) * (1.0 / width)
    for at in range(0, width, LANES):
        span = slice(at, at + LANES)
        normed = tokens_ref[:, span].astype(jnp.float32) * inverse
        out_ref[:, span] = ((grad_ref[:, span] - normed * mixing) * inverse).astype(jnp.bfloat16)


def along_z(v, step):
    size = 2 * NZ
    pairs = []
    for z in range(size):
        for core in range(2):
            to = (z + (step if core == 0 else -step)) % size
            pairs.append([((at % NZ) * 2 + at // NZ) * 2 + core for at in (z, to)])
    return lax.ppermute(v, ("zl", "zh", "core"), pairs)


def along_side(v, step, leg):
    pairs = []
    for y in range(NY):
        for x in range(NX):
            for core in range(2):
                to_y, to_x = (y, (x + step) % NX) if core == leg else ((y + step) % NY, x)
                pairs.append(((y * NX + x) * 2 + core, (to_y * NX + to_x) * 2 + core))
    return lax.ppermute(v, ("y", "x", "core"), pairs)


def swap_cores(v):
    return lax.ppermute(v, "core", [(0, 1), (1, 0)])


def join_kernel(line_ref, ahead_ref, across_ref, back_ref, *plane_refs):
    size = line_ref.shape[1]
    for run, plane_ref in enumerate(plane_refs):
        for i, ref in enumerate((line_ref, ahead_ref, across_ref, back_ref)):
            plane_ref[i * size : (i + 1) * size] = ref[run]


def join(*parts):
    runs, size, *tile = parts[0].shape
    return pl.pallas_call(
        join_kernel,
        out_shape=[pltpu.VMEM((SIDE * size, *tile), parts[0].dtype)] * runs,
        in_specs=[VMEM] * len(parts),
        out_specs=[VMEM] * runs,
        compiler_params=pltpu.CompilerParams(vmem_limit_bytes=1 << 20),
    )(*map(on_chip, parts))


def of_core(table, core):
    paired = table.reshape(*table.shape[:-4], 2, 2, *table.shape[-3:])
    return lax.dynamic_index_in_dim(paired, core, paired.ndim - 4, keepdims=False)


def gather_tiles(own, core, prepare, raw):
    _, slots = own.shape[:2]
    mine = of_core(own, core)
    far = along_z(own, 3)
    middle = along_z(own, 2)
    near = along_z(own, 1)
    opposite = along_z(of_core(middle, core), 2)
    near, middle, far, raw = lax.optimization_barrier((near, middle, far, raw))
    side = jnp.stack([near, middle, far])
    early = prepare(*raw)
    theirs = swap_cores(of_core(side, 1 - core))
    line = jnp.concatenate([mine[None], of_core(side, core), opposite[None], theirs], axis=0)
    line, early = lax.optimization_barrier((line, early))
    line = line.transpose(1, 0, 2, 3, 4).reshape(2, NZ * slots, HALF, 2 * BLOCK)
    across, back, ahead = along_side(line, 2, 0), along_side(line, 1, 0), along_side(line, -1, 0)
    planes = join(line, ahead, across, back)
    back_0, ahead_1 = along_side(planes[0], 1, 1), along_side(planes[1], -1, 1)
    back_1, ahead_0 = along_side(planes[1], 1, 1), along_side(planes[0], -1, 1)
    across_0, across_1 = along_side(back_0, 1, 1), along_side(ahead_1, -1, 1)
    pieces = [planes[0], ahead_0, across_0, back_0, planes[1], ahead_1, across_1, back_1]
    return pieces, early


def tile_places(block_slot, slots, y, zl, x, core):
    owner, place = block_slot // slots, block_slot % slots
    step_x = (owner % NX - x) % NX
    step_z = ((owner // NX) % NZ - zl) * (2 * core - 1) % NZ
    step_z = jnp.where(step_z > NZ // 2, 3 * NZ // 2 - step_z, step_z)
    step_y = (owner // (NX * NZ) - y) % NY
    first = jnp.where(core == 0, step_x, step_y)
    second = jnp.where(core == 0, step_y, step_x)
    return ((second * SIDE + first) * NZ + step_z) * slots + place


def sparse_call(columns, per_column, places, rows, back_places, back_columns, units, mine, other, tiles):
    row_blocks, _, count = mine.shape
    late = (2, SIDE + 2)
    early = [i for i in range(len(tiles)) if i not in late]
    filled = fill_call(early, [tiles[i] for i in early])

    def body(*refs):
        sparse_kernel(columns, per_column, *refs)

    full, grads, send = pl.pallas_call(
        body,
        out_shape=(
            pltpu.VMEM(filled.shape, filled.dtype),
            pltpu.VMEM((2 * columns, BLOCK, 2 * count), jnp.bfloat16),
            pltpu.VMEM((row_blocks, BLOCK, count), jnp.bfloat16),
        ),
        in_specs=[SMEM] * 4 + [VMEM] * 6,
        out_specs=(VMEM, VMEM, VMEM),
        input_output_aliases={7: 0},
        compiler_params=pltpu.CompilerParams(vmem_limit_bytes=3 << 20),
    )(
        places, rows, back_places, back_columns, on_chip(units), on_chip(mine), on_chip(other),
        on_chip(filled), *(on_chip(tiles[i]) for i in late),
    )
    came = swap_cores(send)
    keep = pl.pallas_call(
        keep_kernel,
        out_shape=pltpu.VMEM((row_blocks, BLOCK, count), jnp.float32),
        in_specs=[SMEM] * 2 + [VMEM] * 2,
        out_specs=VMEM,
        compiler_params=pltpu.CompilerParams(vmem_limit_bytes=3 << 20),
    )(back_places, back_columns, on_chip(full), on_chip(grads))
    return keep, came


def norm_call(tokens, gain):
    count, width = tokens.shape
    return pl.pallas_call(
        norm_kernel,
        out_shape=(
            pltpu.VMEM((width, count), jnp.bfloat16),
            pltpu.VMEM((count, 1), jnp.float32),
        ),
        in_specs=[VMEM, VMEM],
        out_specs=(VMEM, VMEM),
        compiler_params=pltpu.CompilerParams(vmem_limit_bytes=6 << 20),
    )(on_chip(tokens), gain)


def close_call(keep, came, tokens, gain, inverse):
    count, width = tokens.shape
    return pl.pallas_call(
        close_kernel,
        out_shape=jax.ShapeDtypeStruct((count, width), jnp.bfloat16),
        in_specs=[VMEM] * 5,
        out_specs=VMEM,
        scratch_shapes=[pltpu.VMEM((count, width), jnp.float32)],
        compiler_params=pltpu.CompilerParams(vmem_limit_bytes=6 << 20),
    )(
        on_chip(keep.reshape(width, count)), on_chip(came.reshape(width, count)), on_chip(tokens),
        gain, on_chip(inverse),
    )


def unit_kernel(high_ref, near_ref, far_ref, units_ref):
    near, far, high = near_ref[...], far_ref[...], high_ref[0]
    groups = near.shape[0] // GROUP
    for run in range(2):
        turned = jnp.where(high == run, near, far).T
        for g in range(groups):
            units_ref[run * groups + g] = turned[:, g * GROUP : (g + 1) * GROUP]


def unit_call(high, near, far):
    columns, block = near.shape
    return pl.pallas_call(
        unit_kernel,
        out_shape=pltpu.VMEM((2 * columns // GROUP, block, GROUP), jnp.float32),
        in_specs=[SMEM, VMEM, VMEM],
        out_specs=VMEM,
        compiler_params=pltpu.CompilerParams(vmem_limit_bytes=1 << 20),
    )(high, on_chip(near), on_chip(far))


def pack_tiles(tiles):
    lead = tiles.shape[:-1]
    split = tiles.reshape(*lead, 2, HALF, BLOCK)
    return jnp.moveaxis(split, -3, -2).reshape(*lead, HALF, 2 * BLOCK)


def on_device(tokens, norm_gain, penalty, weight_tiles, block_rows, block_slot):
    y, zl, x, zh, core = (lax.axis_index(name) for name in AXES)
    runs, slots, _ = weight_tiles.shape
    count, width = tokens.shape
    columns, per_column = block_rows.shape[0] // runs, block_rows.shape[1]

    def of_runs(table):
        paired = table.reshape(2, 2, columns * per_column)
        return lax.dynamic_index_in_dim(paired, core, 1, keepdims=False).reshape(-1)

    def prepare(block_rows, block_slot, penalty):
        places = tile_places(block_slot, slots, y, zl, x, core).reshape(runs, columns * per_column)
        second = jnp.arange(runs)[:, None] // 2 * (NX * NY * NZ * slots)
        return of_runs(block_rows), of_runs(places + second), penalty.reshape(columns, BLOCK), zh.reshape(1)

    own = pack_tiles(weight_tiles)
    raw = block_rows, block_slot, penalty
    tiles, (rows, places, near, high) = gather_tiles(own, core, prepare, raw)
    gain = norm_gain.reshape(1, width)
    features, inverse = norm_call(tokens, gain)
    other = swap_cores(features)
    distant = lax.ppermute(near, "zh", [(0, 1), (1, 0)])
    units = unit_call(high, near, distant)
    blocks = (width // BLOCK, BLOCK, count)
    back = invert_call(columns, per_column, width // BLOCK, places, rows)
    keep, came = sparse_call(
        columns, per_column, places, rows, *back, units, features.reshape(blocks), other.reshape(blocks), tiles
    )
    return close_call(keep, came, tokens, gain, inverse)


def solution(mesh):
    fine = Mesh(mesh.devices.reshape(NY, NZ, NX, 2, 2), AXES)
    placed = (P(AXES, None), P(), P(("zh", "core")), P(None, ("y", "zl", "x"), None), P(), P())

    return jax.shard_map(on_device, mesh=fine, in_specs=placed, out_specs=P(AXES, None), check_vma=False)
```
